128 devices in a mesh: seq: 32 (over x, y, core), head: 4 (over z).
Axes of the slice: x: 4, y: 4, z: 4, core: 2. Of those that a mesh axis runs over, the one named last changes fastest.
Arguments:
- queries: bfloat16 [8192, 64, 128], P('seq', 'head'), may hold values from -200 to 200
- keys: bfloat16 [8192, 8, 128], P('seq', 'head'), may hold values from -8 to 8
- values: bfloat16 [8192, 8, 128], P('seq', 'head'), may hold values from -6 to 6
- query_map: bfloat16 [64, 128, 64], P('head'), may hold values from -40 to 40
- key_map: bfloat16 [8, 128, 64], P('head'), may hold values from -40 to 40
Outputs:
- teacher_attn: bfloat16 [8192, 64, 128], P('seq', 'head')
- student_attn: bfloat16 [8192, 64, 128], P('seq', 'head')
- loss: float32 [], replicated
The draws below stay inside these ranges and needn't reach their ends.
All inputs are finite; a program needn't handle non-finite values.
Results may differ from the reference program's by a relative error of at most 0.01.
Values may be sent and summed in bfloat16 or wider, within the bound.
No kernel may reach another device: no remote copies, remote signals or barrier semaphores. Data moves between devices by JAX's collectives and lax.ppermute only.
A program may use at most 320 MiB of HBM per device.

```python
import jax
import jax.numpy as jnp
from jax import lax

H = 64
KV = 8
HD = 128
FH = 64
TOK_DEV = 256
FEAT = 128
SEQ_LEN = 8192


def query_key_pair(key):
    split_keys = jax.random.split(jax.random.fold_in(key, 7), 2)
    keys = jax.random.normal(split_keys[1], (SEQ_LEN, KV, HD), jnp.float32)
    queries = jax.random.normal(split_keys[0], (SEQ_LEN, H, HD), jnp.float32)
    return (queries, keys)


def feature_map(key, heads):
    split_keys = jax.random.split(key, 1)
    weights = jax.random.normal(split_keys[0], (heads, HD, FH), jnp.float32) / HD ** 0.5
    return weights


def draw_queries(key, part):
    return query_key_pair(key)[0].astype(jnp.bfloat16)


def draw_keys(key, part):
    return query_key_pair(key)[1].astype(jnp.bfloat16)


def draw_query_map(key, part):
    return feature_map(jax.random.fold_in(key, 11), H).astype(jnp.bfloat16)


def draw_key_map(key, part):
    return feature_map(jax.random.fold_in(key, 13), KV).astype(jnp.bfloat16)


def steps_of(own_key, shape, cuts, low, high):
    def one(dim, shards_of):
        heights = jax.random.uniform(jax.random.fold_in(jax.random.fold_in(own_key, 6), dim), (shards_of,), jnp.float32, low / len(cuts), high / len(cuts))
        return jnp.repeat(jnp.exp(heights), shape[dim] // shards_of).reshape((-1,) + (1,) * (len(shape) - dim - 1))

    level = one(*cuts[0])
    for cut in cuts[1:]:
        level = level * one(*cut)
    return level


def centred(key, shape, scale, reach, cuts=(), held_as=jnp.bfloat16):
    array = jax.random.normal(key, shape, jnp.float32) * scale
    if len(cuts) > 0:
        array = steps_of(key, shape, cuts, -0.22, 0.18) * array
    return jnp.clip(array, min=-reach, max=reach).astype(held_as)


def setup_inputs(seed: int = 0) -> dict:
    seeds = jax.random.split(jax.random.key(seed), 6)
    queries = draw_queries(jax.random.fold_in(seeds[5], 71), 0)
    keys = draw_keys(jax.random.fold_in(seeds[5], 71), 0)
    values = centred(seeds[2], (SEQ_LEN, KV, HD), 1.0, 6.0, ((0, 32), (1, 4)))
    query_map = draw_query_map(jax.random.fold_in(seeds[5], 71), 0)
    key_map = draw_key_map(jax.random.fold_in(seeds[5], 71), 0)
    return dict(queries=queries, keys=keys, values=values, query_map=query_map, key_map=key_map)


def features(rows, projection):
    mapped = jnp.einsum('thd,hdf->thf', rows.astype(jnp.float32), projection.astype(jnp.float32))
    both = jnp.concatenate([jax.nn.softmax(mapped, axis=-1), jax.nn.softmax(-mapped, axis=-1)], axis=-1)
    return both.astype(jnp.bfloat16)


def teacher(queries, keys, values):
    group = H // KV
    block = min(512, SEQ_LEN)
    count = SEQ_LEN // block
    scale = 1.0 / (HD ** 0.5)
    grouped = queries.reshape(SEQ_LEN, KV, group, HD).transpose(1, 0, 2, 3).astype(jnp.float32)
    key_rows = keys.transpose(1, 0, 2).astype(jnp.float32)
    value_rows = values.transpose(1, 0, 2).astype(jnp.float32)
    key_pos = jnp.arange(SEQ_LEN, dtype=jnp.int32)

    def single(index):
        head_group = index // count
        first = (index % count) * block
        query_block = lax.dynamic_slice_in_dim(grouped[head_group], first, block, 0)
        scores = jnp.einsum('qsd,kd->sqk', query_block, key_rows[head_group]) * scale
        query_pos = first + jnp.arange(block, dtype=jnp.int32)
        allowed = query_pos[:, None] >= key_pos[None, :]
        scores = jnp.where(allowed[None], scores, -1e30)
        top = jnp.max(scores, axis=-1, keepdims=True)
        weight = jnp.where(allowed[None], jnp.exp(scores - top), 0.0)
        total = jnp.sum(weight, axis=-1)
        mixed = jnp.einsum('sqk,kd->qsd', weight.astype(jnp.bfloat16).astype(jnp.float32), value_rows[head_group])
        return mixed / total.T[:, :, None]

    pieces = lax.map(single, jnp.arange(KV * count, dtype=jnp.int32))
    pieces = pieces.reshape(KV, count, block, group, HD).transpose(1, 2, 0, 3, 4)
    return pieces.reshape(SEQ_LEN, H, HD).astype(jnp.bfloat16)


def student(queries, keys, values, query_map, key_map):
    group = H // KV
    blocks = SEQ_LEN // TOK_DEV
    phi_q = features(queries, query_map).reshape(blocks, TOK_DEV, KV, group, FEAT)
    phi_k = features(keys, key_map).reshape(blocks, TOK_DEV, KV, FEAT)
    value_blocks = values.reshape(blocks, TOK_DEV, KV, HD)
    lower = jnp.tril(jnp.ones((TOK_DEV, TOK_DEV), dtype=bool))

    def advance(carry, inputs):
        state, norm = carry
        pq, pk, vb = inputs
        pqf = pq.astype(jnp.float32)
        pkf = pk.astype(jnp.float32)
        vbf = vb.astype(jnp.float32)
        inner = jnp.einsum('cgsf,egf->gsce', pqf, pkf)
        inner = jnp.where(lower[None, None], inner, 0.0)
        den_local = jnp.sum(inner, axis=-1)
        num_local = jnp.einsum('gsce,egd->cgsd', inner.astype(jnp.bfloat16).astype(jnp.float32), vbf)
        state_round = lax.optimization_barrier(state.astype(jnp.bfloat16)).astype(jnp.float32)
        num_prev = jnp.einsum('cgsf,gfd->cgsd', pqf, state_round)
        den_prev = jnp.einsum('cgsf,gf->gsc', pqf, norm, precision=lax.Precision.HIGHEST)
        denom = (den_local + den_prev).transpose(2, 0, 1)[..., None]
        result = ((num_local + num_prev) / denom).astype(jnp.bfloat16)
        state = state + jnp.einsum('cgf,cgd->gfd', pkf, vbf)
        norm = norm + jnp.sum(pkf, axis=0)
        return (state, norm), result

    start = (jnp.zeros((KV, FEAT, HD), jnp.float32), jnp.zeros((KV, FEAT), jnp.float32))
    _, outputs = lax.scan(advance, start, (phi_q, phi_k, value_blocks))
    return outputs.reshape(SEQ_LEN, H, HD)


def reference(queries, keys, values, query_map, key_map):
    teacher_attn = teacher(queries, keys, values)
    student_attn = student(queries, keys, values, query_map, key_map)
    diff = teacher_attn.astype(jnp.float32) - student_attn.astype(jnp.float32)
    loss = jnp.sum(diff * diff) / (SEQ_LEN * H * HD)
    return teacher_attn, student_attn, loss
```

```python
import functools

import jax
import jax.numpy as jnp
import numpy as np
from jax import lax
from jax.experimental import pallas as pl
from jax.experimental.pallas import tpu as pltpu
from jax.sharding import Mesh
from jax.sharding import PartitionSpec as P


SEQ = ("x", "y", "c")
BF = jnp.bfloat16
F32 = jnp.float32
NT = (((1,), (1,)), ((), ()))
BLK = 256
SUB = 1024

ORDERS = {
    (0, 0): ("x1", "y1", "x3", "y3"),
    (0, 1): ("y1", "x3", "y3", "x1"),
    (1, 0): ("x3", "y3", "x1", "y1"),
    (1, 1): ("y3", "x1", "y1", "x3"),
}
MASK = {"x1": 4, "x3": 12, "y1": 1, "y3": 3}


def block_table():
    table = np.zeros((16, 2, 2, 16), np.int32)
    for (core, half), order in ORDERS.items():
        for place in range(16):
            mask = 0
            for step, name in enumerate(order):
                if place >> step & 1:
                    mask ^= MASK[name]
            for chip in range(16):
                table[chip, core, half, chip ^ mask] = place
    return table


TABLE = block_table()


def permute(value, axes, target):
    pairs = []
    for chip in range(16):
        for core in range(2):
            to = target(chip, core)
            if to is not None:
                pairs.append((chip * 2 + core, to[0] * 2 + to[1]))
    return lax.ppermute(value, axes, pairs)


def features(mapped):
    high = jnp.max(mapped, axis=0, keepdims=True)
    low = jnp.min(mapped, axis=0, keepdims=True)
    up = jnp.exp(mapped - high)
    down = jnp.exp(low - mapped)
    up = up * (1.0 / jnp.sum(up, axis=0, keepdims=True))
    down = down * (1.0 / jnp.sum(down, axis=0, keepdims=True))
    return jnp.concatenate([up, down], axis=0).astype(BF)


def block_at(ref, index):
    return pl.ds(pl.multiple_of(index * BLK, BLK), BLK)


def student_kernel(tab, x_ref, y_ref, ga, gb, wk, wq, sx_ref, sy_ref, stx, sty, nx, ny):
    chip = tab[32]
    far = 15 - chip
    stx[...] = jnp.zeros_like(stx)
    sty[...] = jnp.zeros_like(sty)
    nx[...] = jnp.zeros_like(nx)
    ny[...] = jnp.zeros_like(ny)
    ones = jnp.ones((8, BLK), BF)

    def add(j, _):
        rows_a = block_at(ga, tab[j])
        rows_b = block_at(gb, tab[16 + j])
        k = jnp.concatenate([ga[rows_a, :128], gb[rows_b, :128]], axis=0)
        phi = features(lax.dot_general(wk[...], k, NT, preferred_element_type=F32))
        phi_a, phi_b = phi[:, :BLK], phi[:, BLK:]
        state_a = jnp.dot(phi_a, ga[rows_a, 128:], preferred_element_type=F32)
        state_b = jnp.dot(phi_b, gb[rows_b, 128:], preferred_element_type=F32)
        norm_a = lax.dot_general(ones, phi_a, NT, preferred_element_type=F32)
        norm_b = lax.dot_general(ones, phi_b, NT, preferred_element_type=F32)
        in_x = jnp.where(j < chip, 1.0, 0.0).astype(F32)
        in_ya = jnp.where(j <= far, 1.0, 0.0).astype(F32)
        in_yb = jnp.where(j < far, 1.0, 0.0).astype(F32)
        stx[...] += in_x * (state_a + state_b)
        nx[...] += in_x * (norm_a + norm_b)
        sty[...] += in_ya * state_a + in_yb * state_b
        ny[...] += in_ya * norm_a + in_yb * norm_b
        return 0

    lax.fori_loop(0, jnp.maximum(chip, far + 1), add, 0)

    def segment(q_ref, keys, values, state, norm, out_ref):
        phi_k = features(lax.dot_general(wk[...], keys, NT, preferred_element_type=F32))
        state_b = state[...].astype(BF)
        norm_row = norm[0:1, :]
        rows = lax.broadcasted_iota(jnp.int32, (BLK, BLK), 0)
        cols = lax.broadcasted_iota(jnp.int32, (BLK, BLK), 1)

        def head(h, _):
            place = block_at(q_ref, h)
            mapped = lax.dot_general(wq[h], q_ref[place, :], NT, preferred_element_type=F32)
            phi_q = features(mapped).T
            inner = jnp.dot(phi_q, phi_k, preferred_element_type=F32)
            inner = jnp.where(rows >= cols, inner, 0.0)
            num = jnp.dot(inner.astype(BF), values, preferred_element_type=F32)
            num = num + jnp.dot(phi_q, state_b, preferred_element_type=F32)
            den = inner[:, :128] + inner[:, 128:] + phi_q.astype(F32) * norm_row
            den = jnp.sum(den, axis=-1, keepdims=True)
            out_ref[place, :] = (num / den).astype(BF)
            return 0

        lax.fori_loop(0, 8, head, 0)

    own = block_at(ga, tab[chip])
    segment(x_ref, ga[own, :128], ga[own, 128:], stx, nx, sx_ref)
    own = block_at(gb, tab[16 + far])
    segment(y_ref, gb[own, :128], gb[own, 128:], sty, ny, sy_ref)


def teacher_kernel(
    tab, x_ref, y_ref, ga, gb, sx_ref, sy_ref, ox_ref, oy_ref, part_ref, top_s, sum_s, acc_s
):
    chip = tab[32]
    far = 15 - chip
    unit = 1.4426950408889634 / 128**0.5
    part_ref[...] = jnp.zeros_like(part_ref)

    def tile(q_ref, piece, k, v, diagonal, first):
        rows = slice(piece * SUB, (piece + 1) * SUB)
        wide = k.shape[0] // 128
        s = lax.dot_general(q_ref[rows, :], k, NT, preferred_element_type=F32) * unit
        if diagonal:
            shape = (SUB, BLK)
            row = lax.broadcasted_iota(jnp.int32, shape, 0) & (BLK - 1)
            last = jnp.where(row >= lax.broadcasted_iota(jnp.int32, shape, 1), s[:, -BLK:], -1e30)
            s = last if wide == 2 else jnp.concatenate([s[:, :-BLK], last], axis=1)
        peak = jnp.broadcast_to(jnp.max(s, axis=-1, keepdims=True), (SUB, 128))
        top = peak if first else jnp.maximum(top_s[rows, :], peak)
        p = jnp.exp2(s - jnp.concatenate([top] * wide, axis=1))
        added = p[:, :128]
        for i in range(1, wide):
            added = added + p[:, i * 128 : (i + 1) * 128]
        mixed = jnp.dot(p.astype(BF), v, preferred_element_type=F32)
        if first:
            sum_s[rows, :] = added
            acc_s[rows, :] = mixed
        else:
            keep = jnp.exp2(top_s[rows, :] - top)
            sum_s[rows, :] = sum_s[rows, :] * keep + added
            acc_s[rows, :] = acc_s[rows, :] * keep + mixed
        top_s[rows, :] = top

    def both(ref_a, ref_b, index, lanes):
        a = ref_a[block_at(ref_a, tab[index]), lanes]
        b = ref_b[block_at(ref_b, tab[16 + index]), lanes]
        return jnp.concatenate([a, b], axis=0)

    def segment(q_ref, k, v, count, s_ref, o_ref):
        for piece in range(2):
            tile(q_ref, piece, k, v, True, True)

        def step(j, _):
            k = both(ga, gb, j, slice(0, 128))
            v = both(ga, gb, j, slice(128, 256))
            for piece in range(2):
                tile(q_ref, piece, k, v, False, False)
            return 0

        lax.fori_loop(0, count, step, 0)
        for piece in range(2):
            rows = slice(piece * SUB, (piece + 1) * SUB)
            total = jnp.sum(sum_s[rows, :], axis=-1, keepdims=True)
            out = (acc_s[rows, :] / total).astype(BF)
            o_ref[rows, :] = out
            diff = out.astype(F32) - s_ref[rows, :].astype(F32)
            part_ref[...] += jnp.sum((diff * diff).reshape(SUB // 8, 8, 128), axis=0)

    own = block_at(ga, tab[chip])
    segment(x_ref, ga[own, :128], ga[own, 128:], chip, sx_ref, ox_ref)
    segment(
        y_ref,
        both(ga, gb, far, slice(0, 128)),
        both(ga, gb, far, slice(128, 256)),
        far,
        sy_ref,
        oy_ref,
    )
    part_ref[...] = jnp.full_like(part_ref, jnp.sum(part_ref[...]))


def call(kernel, name, outs, scratch, flops, args):
    vmem = pl.BlockSpec(memory_space=pltpu.VMEM)
    return pl.pallas_call(
        kernel,
        name=name,
        out_shape=outs,
        in_specs=[pl.BlockSpec(memory_space=pltpu.SMEM)] + [vmem] * (len(args) - 1),
        out_specs=[vmem] * len(outs),
        scratch_shapes=[pltpu.VMEM(shape, F32) for shape in scratch],
        compiler_params=pltpu.CompilerParams(vmem_limit_bytes=48 << 20),
        cost_estimate=pl.CostEstimate(flops=flops, bytes_accessed=6 << 20, transcendentals=0),
    )(*args)


def local(queries, keys, values, query_map, key_map):
    rows, heads, size = queries.shape
    core = lax.axis_index("c")
    chip = lax.axis_index("x") * 4 + lax.axis_index("y")
    first = core == 0
    pick = lambda a, b: jnp.where(first, a, b)

    kv = [jnp.concatenate([keys[:, g], values[:, g]], axis=1) for g in range(2)]
    kv_same, kv_other = pick(kv[0], kv[1]), pick(kv[1], kv[0])
    q = queries.transpose(1, 0, 2).reshape(2, heads // 2 * rows, size)
    q_same, q_other = pick(q[0], q[1]), pick(q[1], q[0])

    kv_came = permute(kv_other, SEQ, lambda r, c: (r, 1 - c))
    gathered = [pick(kv_same, kv_came), pick(kv_came, kv_same)]
    q_came = permute(q_other, SEQ, lambda r, c: (r, 1) if c == 0 else (15 - r, 0))
    q_far = permute(q_same, SEQ, lambda r, c: None if c == 0 else (15 - r, 1))
    x = pick(q_same, q_came)
    y = pick(q_came, q_far)

    for step in range(4):
        came = [
            permute(
                gathered[half],
                SEQ,
                lambda r, c: (r ^ MASK[ORDERS[c, half][step]], c),
            )
            for half in range(2)
        ]
        gathered = [jnp.concatenate([g, n], axis=0) for g, n in zip(gathered, came)]

    table = lax.dynamic_slice(
        jnp.asarray(TABLE.reshape(32, 32)), (chip * 2 + core, 0), (1, 32)
    ).reshape(32)
    table = jnp.concatenate([table, chip.reshape(1).astype(jnp.int32)])
    wk = lax.dynamic_index_in_dim(key_map, core, 0, keepdims=False).T
    wq = lax.dynamic_slice_in_dim(query_map, core * 8, 8, 0).transpose(0, 2, 1)

    shape = jax.ShapeDtypeStruct(x.shape, BF)
    sx, sy = call(
        student_kernel,
        "student",
        [shape, shape],
        [(128, 128), (128, 128), (8, 128), (8, 128)],
        3_000_000_000,
        (table, x, y, *gathered, wk, wq),
    )

    def send_back(near, distant):
        came = permute(
            pick(distant, near), SEQ, lambda r, c: (r, 0) if c == 1 else (15 - r, 1)
        )
        came_far = permute(distant, SEQ, lambda r, c: None if c == 0 else (15 - r, 1))
        same = pick(near, came_far)
        return pick(same, came), pick(came, same)

    def assemble(low, high):
        whole = jnp.concatenate([low, high], axis=0).reshape(heads, rows, size)
        return whole.transpose(1, 0, 2)

    student_pair = send_back(sx, sy)
    ox, oy, part = call(
        teacher_kernel,
        "teacher",
        [shape, shape, jax.ShapeDtypeStruct((8, 128), F32)],
        [(2 * SUB, 128)] * 3,
        9_000_000_000,
        (table, x, y, *gathered, sx, sy),
    )
    teacher_pair = send_back(ox, oy)
    part = part + permute(part, SEQ, lambda r, c: (r, 1 - c))
    for mask in (4, 12, 1, 3):
        part = part + permute(part, SEQ, lambda r, c: (r ^ mask, c))
    for mask in (1, 3):
        part = part + lax.ppermute(part, "h", [(z, z ^ mask) for z in range(4)])
    loss = part[0, 0] / (16 * 2 * rows * heads * lax.axis_size("h") * size)
    return assemble(*teacher_pair), assemble(*student_pair), loss


def solution(mesh):
    torus = Mesh(mesh.devices.reshape(4, 4, 2, mesh.shape["head"]), ("x", "y", "c", "h"))
    return jax.shard_map(
        local,
        mesh=torus,
        in_specs=(
            P(SEQ, "h", None),
            P(SEQ, "h", None),
            P(SEQ, "h", None),
            P("h", None, None),
            P("h", None, None),
        ),
        out_specs=(P(SEQ, "h", None), P(SEQ, "h", None), P()),
        check_vma=False,
    )
```

```python
import jax
import jax.numpy as jnp
import numpy as np
from jax import lax
from jax.experimental import pallas as pl
from jax.experimental.pallas import tpu as pltpu
from jax.sharding import Mesh
from jax.sharding import PartitionSpec as P


SEQ = ("x", "y", "c")
BF = jnp.bfloat16
F32 = jnp.float32
NT = (((1,), (1,)), ((), ()))
BLK = 256
SUB = 1024

OFFSETS = (0, 3, 1, 2)


def slot_table():
    table = np.zeros((16, 2, 16), np.int32)
    for chip in range(16):
        for slot in range(16):
            one, two = OFFSETS[slot % 4], OFFSETS[slot // 4]
            for core, (dx, dy) in enumerate(((one, two), (two, one))):
                table[chip, core, slot] = moved(chip, dx, dy)
    return table


def moved(chip, dx, dy):
    return (chip // 4 + dx) % 4 * 4 + (chip + dy) % 4


TABLE = slot_table()


def permute(value, axes, target):
    pairs = []
    for chip in range(16):
        for core in range(2):
            to = target(chip, core)
            if to is not None:
                pairs.append((chip * 2 + core, to[0] * 2 + to[1]))
    return lax.ppermute(value, axes, pairs)


def features(mapped):
    high = jnp.max(mapped, axis=0, keepdims=True)
    low = jnp.min(mapped, axis=0, keepdims=True)
    up = jnp.exp(mapped - high)
    down = jnp.exp(low - mapped)
    up = up * (1.0 / jnp.sum(up, axis=0, keepdims=True))
    down = down * (1.0 / jnp.sum(down, axis=0, keepdims=True))
    return jnp.concatenate([up, down], axis=0).astype(BF)


def block_at(index, size=BLK):
    return pl.ds(pl.multiple_of(index * size, size), size)


def student_inside(q_ref, keys, values, wk, wq, phi_ref, num_ref, den_ref):
    phi_k = features(lax.dot_general(wk[...], keys, NT, preferred_element_type=F32))
    rows = lax.broadcasted_iota(jnp.int32, (BLK, BLK), 0)
    cols = lax.broadcasted_iota(jnp.int32, (BLK, BLK), 1)

    def head(h, _):
        place = block_at(h)
        mapped = lax.dot_general(wq[h], q_ref[place, :], NT, preferred_element_type=F32)
        phi_q = features(mapped).T
        inner = jnp.dot(phi_q, phi_k, preferred_element_type=F32)
        inner = jnp.where(rows >= cols, inner, 0.0)
        phi_ref[place, :] = phi_q
        num_ref[place, :] = jnp.dot(inner.astype(BF), values, preferred_element_type=F32)
        den_ref[place, :] = inner[:, :128] + inner[:, 128:]
        return 0

    lax.fori_loop(0, 8, head, 0, unroll=2)


def near_kernel(x_ref, kv, wk, wq, phi_ref, num_ref, den_ref):
    student_inside(x_ref, kv[:, :128], kv[:, 128:], wk, wq, phi_ref, num_ref, den_ref)


def add_state(tab, wk, slot, kv, stx, sty, nx, ny):
    chip = tab[16]
    far = 15 - chip
    other = tab[slot]
    ones = jnp.ones((8, BLK), BF)
    phi = features(lax.dot_general(wk[...], kv[:, :128], NT, preferred_element_type=F32))
    phi_a, phi_b = phi[:, :BLK], phi[:, BLK:]
    state_a = jnp.dot(phi_a, kv[:BLK, 128:], preferred_element_type=F32)
    state_b = jnp.dot(phi_b, kv[BLK:, 128:], preferred_element_type=F32)
    norm_a = lax.dot_general(ones, phi_a, NT, preferred_element_type=F32)
    norm_b = lax.dot_general(ones, phi_b, NT, preferred_element_type=F32)
    in_x = jnp.where(other < chip, 1.0, 0.0).astype(F32)
    in_ya = jnp.where(other <= far, 1.0, 0.0).astype(F32)
    in_yb = jnp.where(other < far, 1.0, 0.0).astype(F32)
    stx[...] += in_x * (state_a + state_b)
    nx[...] += in_x * (norm_a + norm_b)
    sty[...] += in_ya * state_a + in_yb * state_b
    ny[...] += in_ya * norm_a + in_yb * norm_b


def far_kernel(tab, y_ref, own, wk, wq, phi_ref, num_ref, den_ref, stx, sty, nx, ny):
    for ref in (stx, sty, nx, ny):
        ref[...] = jnp.zeros_like(ref)
    for i in range(4):
        add_state(tab, wk, i, own[i * 2 * BLK : (i + 1) * 2 * BLK, :], stx, sty, nx, ny)
    keys, values = y_ref[8 * BLK : 9 * BLK, :], y_ref[9 * BLK :, :]
    student_inside(y_ref, keys, values, wk, wq, phi_ref, num_ref, den_ref)


def middle_kernel(tab, left, right, wk, stx0, sty0, nx0, ny0, stx, sty, nx, ny):
    for ref, start in ((stx, stx0), (sty, sty0), (nx, nx0), (ny, ny0)):
        ref[...] = start[...]
    for group, ref in enumerate((left, right)):
        for i in range(4):
            kv = ref[i * 2 * BLK : (i + 1) * 2 * BLK, :]
            add_state(tab, wk, 4 + group * 4 + i, kv, stx, sty, nx, ny)


def finish_kernel(
    tab, opp0, opp1, wk, stx0, sty0, nx0, ny0, phi_x, num_x, den_x, phi_y, num_y, den_y,
    sx_ref, sy_ref, stx, sty, nx, ny,
):
    for ref, start in ((stx, stx0), (sty, sty0), (nx, nx0), (ny, ny0)):
        ref[...] = start[...]
    for group, ref in enumerate((opp0, opp1)):
        for i in range(2):
            kv = ref[i * 2 * BLK : (i + 1) * 2 * BLK, :]
            add_state(tab, wk, 12 + group * 2 + i, kv, stx, sty, nx, ny)
    for phi, num, den, state, norm, out in (
        (phi_x, num_x, den_x, stx, nx, sx_ref),
        (phi_y, num_y, den_y, sty, ny, sy_ref),
    ):
        state_b = state[...].astype(BF)
        norm_row = norm[0:1, :]
        for piece in range(4):
            rows = slice(piece * 512, (piece + 1) * 512)
            phi_q = phi[rows, :]
            top = num[rows, :] + jnp.dot(phi_q, state_b, preferred_element_type=F32)
            low = den[rows, :] + phi_q.astype(F32) * norm_row
            out[rows, :] = (top / jnp.sum(low, axis=-1, keepdims=True)).astype(BF)


def teacher_kernel(
    tab, x_ref, y_ref, own, left, right, opp0, opp1, sx_ref, sy_ref,
    ox_ref, oy_ref, loss_ref, kv_s, part_ref, top_s, sum_s, acc_s, sems,
):
    chip = tab[16]
    far = 15 - chip
    copies = []
    for ref in (own, left, right, opp0, opp1):
        for i in range(ref.shape[0] // (2 * BLK)):
            slot = len(copies)
            copies.append(
                pltpu.make_async_copy(
                    ref.at[pl.ds(i * 2 * BLK, 2 * BLK), :],
                    kv_s.at[block_at(tab[slot], 2 * BLK), :],
                    sems.at[slot],
                )
            )
    for copy in copies:
        copy.start()
    unit = 1.4426950408889634 / 128**0.5
    part_ref[...] = jnp.zeros_like(part_ref)

    def tile(q_ref, piece, k, v, diagonal, first):
        rows = slice(piece * SUB, (piece + 1) * SUB)
        wide = k.shape[0] // 128
        s = lax.dot_general(q_ref[rows, :], k, NT, preferred_element_type=F32) * unit
        if diagonal:
            shape = (SUB, BLK)
            row = lax.broadcasted_iota(jnp.int32, shape, 0) & (BLK - 1)
            last = jnp.where(row >= lax.broadcasted_iota(jnp.int32, shape, 1), s[:, -BLK:], -1e30)
            s = last if wide == 2 else jnp.concatenate([s[:, :-BLK], last], axis=1)
        peak = jnp.broadcast_to(jnp.max(s, axis=-1, keepdims=True), (SUB, 128))
        top = peak if first else jnp.maximum(top_s[rows, :], peak)
        p = jnp.exp2(s - jnp.concatenate([top] * wide, axis=1))
        added = p[:, :128]
        for i in range(1, wide):
            added = added + p[:, i * 128 : (i + 1) * 128]
        mixed = jnp.dot(p.astype(BF), v, preferred_element_type=F32)
        if first:
            sum_s[rows, :] = added
            acc_s[rows, :] = mixed
        else:
            keep = jnp.exp2(top_s[rows, :] - top)
            sum_s[rows, :] = sum_s[rows, :] * keep + added
            acc_s[rows, :] = acc_s[rows, :] * keep + mixed
        top_s[rows, :] = top

    def segment(q_ref, k, v, count, s_ref, o_ref):
        for piece in range(2):
            tile(q_ref, piece, k, v, True, True)

        def step(j, _):
            place = block_at(j, 2 * BLK)
            k, v = kv_s[place, :128], kv_s[place, 128:]
            for piece in range(2):
                tile(q_ref, piece, k, v, False, False)
            return 0

        lax.fori_loop(0, count, step, 0)
        for piece in range(2):
            rows = slice(piece * SUB, (piece + 1) * SUB)
            total = jnp.sum(sum_s[rows, :], axis=-1, keepdims=True)
            out = (acc_s[rows, :] / total).astype(BF)
            o_ref[rows, :] = out
            diff = out.astype(F32) - s_ref[rows, :].astype(F32)
            part_ref[...] += jnp.sum((diff * diff).reshape(SUB // 8, 8, 128), axis=0)

    for copy in copies:
        copy.wait()
    place = block_at(chip * 2)
    segment(x_ref, kv_s[place, :128], kv_s[place, 128:], chip, sx_ref, ox_ref)
    place = block_at(far, 2 * BLK)
    segment(y_ref, kv_s[place, :128], kv_s[place, 128:], far, sy_ref, oy_ref)
    loss_ref[...] = jnp.full_like(loss_ref, jnp.sum(part_ref[...]))


def call(kernel, args, outs, scratch=(), flops=0, table=True, anywhere=(), limit=24):
    vmem = pl.BlockSpec(memory_space=pltpu.VMEM)
    specs = [
        pl.BlockSpec(memory_space=pltpu.SMEM)
        if table and i == 0
        else pl.BlockSpec(memory_space=pl.ANY)
        if i in anywhere
        else vmem
        for i in range(len(args))
    ]
    return pl.pallas_call(
        kernel,
        out_shape=[jax.ShapeDtypeStruct(shape, kind) for shape, kind in outs],
        in_specs=specs,
        out_specs=[vmem] * len(outs),
        scratch_shapes=list(scratch),
        compiler_params=pltpu.CompilerParams(vmem_limit_bytes=limit << 20),
        cost_estimate=pl.CostEstimate(flops=flops, bytes_accessed=1 << 20, transcendentals=0),
    )(*args)


def body(queries, keys, values, query_map, key_map):
    rows, heads, size = queries.shape
    core = lax.axis_index("c")
    chip = lax.axis_index("x") * 4 + lax.axis_index("y")
    first = core == 0
    pick = lambda a, b: jnp.where(first, a, b)

    kv = [jnp.concatenate([keys[:, g], values[:, g]], axis=1) for g in range(2)]
    kv_same, kv_other = pick(kv[0], kv[1]), pick(kv[1], kv[0])
    q = queries.transpose(1, 0, 2).reshape(2, heads // 2 * rows, size)
    q_same, q_other = pick(q[0], q[1]), pick(q[1], q[0])

    kv_came = permute(kv_other, SEQ, lambda r, c: (r, 1 - c))
    q_came = permute(q_other, SEQ, lambda r, c: (r, 1) if c == 0 else None)
    x = pick(q_same, q_came)

    def with_kv(part, pair):
        return jnp.concatenate([part, pair[:, :size], pair[:, size:]], axis=0)

    y_a = permute(
        with_kv(q_other, kv_other), SEQ, lambda r, c: None if c == 0 else (15 - r, 0)
    )
    y_b = permute(
        with_kv(q_same, kv_same), SEQ, lambda r, c: None if c == 0 else (15 - r, 1)
    )
    y = pick(y_a, y_b)
    kv_near = pick(kv_same, kv_came)
    shard = jnp.concatenate([kv_near, pick(kv_came, kv_same)], axis=0)

    def shift(value, phase, by):
        def target(r, c):
            along_x = (c == 0) == (phase == 1)
            return (moved(r, by, 0) if along_x else moved(r, 0, by)), c

        return permute(value, SEQ, target)

    wk = lax.dynamic_index_in_dim(key_map, core, 0, keepdims=False).T
    wq = lax.dynamic_slice_in_dim(query_map, core * 8, 8, 0).transpose(0, 2, 1)
    many = x.shape
    inside = [(many, BF), (many, F32), (many, F32)]
    states = [((128, 128), F32), ((128, 128), F32), ((8, 128), F32), ((8, 128), F32)]

    near_pieces = [shard] + [shift(shard, 1, by) for by in (1, 3, 2)]
    near = call(near_kernel, (x, kv_near, wk, wq), inside, flops=1 << 30, table=False)
    own = jnp.concatenate(near_pieces, axis=0)
    left, right = shift(own, 2, 1), shift(own, 2, 3)
    half = own.shape[0] // 2
    opp0 = shift(left[:half], 2, 1)
    opp1 = shift(right[half:], 2, 3)

    table = lax.dynamic_slice(
        jnp.asarray(TABLE.reshape(32, 16)), (chip * 2 + core, 0), (1, 16)
    ).reshape(16)
    table = jnp.concatenate([table, chip.reshape(1).astype(jnp.int32)])
    *far, stx, sty, nx, ny = call(
        far_kernel, (table, y, own, wk, wq), inside + states, flops=2 << 30
    )
    stx, sty, nx, ny = call(
        middle_kernel, (table, left, right, wk, stx, sty, nx, ny), states, flops=1 << 30
    )
    sx, sy = call(
        finish_kernel,
        (table, opp0, opp1, wk, stx, sty, nx, ny, *near, *far),
        [(many, BF)] * 2,
        [pltpu.VMEM(shape, kind) for shape, kind in states],
        flops=1 << 30,
    )

    def send_back(near, distant):
        came = permute(
            pick(distant, near), SEQ, lambda r, c: (r, 0) if c == 1 else (15 - r, 1)
        )
        came_far = permute(distant, SEQ, lambda r, c: None if c == 0 else (15 - r, 1))
        same = pick(near, came_far)
        return pick(same, came), pick(came, same)

    def assemble(low, high):
        whole = jnp.concatenate([low, high], axis=0).reshape(heads, rows, size)
        return whole.transpose(1, 0, 2)

    student_pair = send_back(sx, sy)
    peers = 32 * lax.axis_size("h")
    ox, oy, part = call(
        teacher_kernel,
        (table, x, y, own, left, right, opp0, opp1, sx, sy),
        [(many, BF), (many, BF), ((peers, 1, 128), F32)],
        [pltpu.VMEM((16 * 2 * BLK, 256), BF), pltpu.VMEM((8, 128), F32)]
        + [pltpu.VMEM((2 * SUB, 128), F32)] * 3
        + [pltpu.SemaphoreType.DMA((16,))],
        flops=9 << 30,
        anywhere=(3, 4, 5, 6, 7),
        limit=32,
    )
    teacher_pair = send_back(ox, oy)

    parts = lax.all_to_all(part, SEQ + ("h",), 0, 0, tiled=True)
    loss = jnp.sum(parts[:, 0, 0]) / (16 * 2 * rows * heads * lax.axis_size("h") * size)
    return assemble(*teacher_pair), assemble(*student_pair), loss


def solution(mesh):
    torus = Mesh(mesh.devices.reshape(4, 4, 2, mesh.shape["head"]), ("x", "y", "c", "h"))
    return jax.shard_map(
        body,
        mesh=torus,
        in_specs=(
            P(SEQ, "h", None),
            P(SEQ, "h", None),
            P(SEQ, "h", None),
            P("h", None, None),
            P("h", None, None),
        ),
        out_specs=(P(SEQ, "h", None), P(SEQ, "h", None), P()),
        check_vma=False,
    )
```

```python
import jax
import jax.numpy as jnp
import numpy as np
from jax import lax
from jax.experimental import pallas as pl
from jax.experimental.pallas import tpu as pltpu
from jax.sharding import Mesh
from jax.sharding import PartitionSpec as P


SEQ = ("x", "y", "c")
BF = jnp.bfloat16
F32 = jnp.float32
NT = (((1,), (1,)), ((), ()))
BLK = 256
SUB = 1024

MASKS = (0, 1, 3, 2)


def moved(chip, mx, my):
    return chip ^ (mx * 4 + my)


def slot_table():
    table = np.zeros((16, 2, 16), np.int32)
    for chip in range(16):
        for slot in range(16):
            one, two = MASKS[slot % 4], MASKS[slot // 4]
            for core, (mx, my) in enumerate(((one, two), (two, one))):
                table[chip, core, slot] = moved(chip, mx, my)
    return table


TABLE = slot_table()


def permute(value, axes, target):
    pairs = []
    for chip in range(16):
        for core in range(2):
            to = target(chip, core)
            if to is not None:
                pairs.append((chip * 2 + core, to[0] * 2 + to[1]))
    return lax.ppermute(value, axes, pairs)


def features(mapped):
    high = jnp.max(mapped, axis=0, keepdims=True)
    low = jnp.min(mapped, axis=0, keepdims=True)
    up = jnp.exp(mapped - high)
    down = jnp.exp(low - mapped)
    up = up * (1.0 / jnp.sum(up, axis=0, keepdims=True))
    down = down * (1.0 / jnp.sum(down, axis=0, keepdims=True))
    return jnp.concatenate([up, down], axis=0).astype(BF)


def block_at(index, size=BLK):
    return pl.ds(pl.multiple_of(index * size, size), size)


def student_inside(q_ref, keys, values, wk, wq, phi_ref, num_ref, den_ref, wide_s):
    wide_s[...] = q_ref[: 8 * BLK, :].astype(F32)
    phi_k = features(lax.dot_general(wk[...], keys, NT, preferred_element_type=F32))
    rows = lax.broadcasted_iota(jnp.int32, (BLK, BLK), 0)
    cols = lax.broadcasted_iota(jnp.int32, (BLK, BLK), 1)

    def head(h, _):
        place = pl.ds(h, BLK, stride=8)
        q = wide_s[place, :].astype(BF)
        mapped = lax.dot_general(wq[h], q, NT, preferred_element_type=F32)
        phi_q = features(mapped).T
        inner = jnp.dot(phi_q, phi_k, preferred_element_type=F32)
        inner = jnp.where(rows >= cols, inner, 0.0)
        phi_ref[place, :] = phi_q.astype(F32)
        num_ref[place, :] = jnp.dot(inner.astype(BF), values, preferred_element_type=F32)
        den_ref[place, :] = inner[:, :128] + inner[:, 128:]
        return 0

    lax.fori_loop(0, 8, head, 0, unroll=2)


def add_state(tab, wk, slot, kv, stx, sty, nx, ny):
    chip = tab[16]
    far = 15 - chip
    other = tab[slot]
    ones = jnp.ones((8, BLK), BF)
    phi = features(lax.dot_general(wk[...], kv[:, :128], NT, preferred_element_type=F32))
    phi_a, phi_b = phi[:, :BLK], phi[:, BLK:]
    state_a = jnp.dot(phi_a, kv[:BLK, 128:], preferred_element_type=F32)
    state_b = jnp.dot(phi_b, kv[BLK:, 128:], preferred_element_type=F32)
    norm_a = lax.dot_general(ones, phi_a, NT, preferred_element_type=F32)
    norm_b = lax.dot_general(ones, phi_b, NT, preferred_element_type=F32)
    in_x = jnp.where(other < chip, 1.0, 0.0).astype(F32)
    in_ya = jnp.where(other <= far, 1.0, 0.0).astype(F32)
    in_yb = jnp.where(other < far, 1.0, 0.0).astype(F32)
    stx[...] += in_x * (state_a + state_b)
    nx[...] += in_x * (norm_a + norm_b)
    sty[...] += in_ya * state_a + in_yb * state_b
    ny[...] += in_ya * norm_a + in_yb * norm_b


def near_kernel(
    tab, x_ref, own, wk, wq, phi_ref, num_ref, den_ref, stx, sty, nx, ny, wide_s
):
    for ref in (stx, sty, nx, ny):
        ref[...] = jnp.zeros_like(ref)
    for i in range(4):
        add_state(tab, wk, i, own[i * 2 * BLK : (i + 1) * 2 * BLK, :], stx, sty, nx, ny)
    keys, values = own[:BLK, :128], own[:BLK, 128:]
    student_inside(x_ref, keys, values, wk, wq, phi_ref, num_ref, den_ref, wide_s)


def far_kernel(
    tab, y_ref, left, right, wk, wq, stx0, sty0, nx0, ny0,
    phi_ref, num_ref, den_ref, stx, sty, nx, ny, wide_s,
):
    own = slice(5 * BLK, 6 * BLK)
    keys, values = right[own, :128], right[own, 128:]
    student_inside(y_ref, keys, values, wk, wq, phi_ref, num_ref, den_ref, wide_s)
    for ref, start in ((stx, stx0), (sty, sty0), (nx, nx0), (ny, ny0)):
        ref[...] = start[...]
    for group, ref in enumerate((left, right)):
        for i in range(4):
            kv = ref[i * 2 * BLK : (i + 1) * 2 * BLK, :]
            add_state(tab, wk, 4 + group * 4 + i, kv, stx, sty, nx, ny)


def finish_kernel(
    tab, opp0, opp1, wk, stx0, sty0, nx0, ny0, phi_x, num_x, den_x, phi_y, num_y, den_y,
    sx_ref, sy_ref, stx, sty, nx, ny,
):
    for ref, start in ((stx, stx0), (sty, sty0), (nx, nx0), (ny, ny0)):
        ref[...] = start[...]
    for group, ref in enumerate((opp0, opp1)):
        for i in range(2):
            kv = ref[i * 2 * BLK : (i + 1) * 2 * BLK, :]
            add_state(tab, wk, 12 + group * 2 + i, kv, stx, sty, nx, ny)
    for phi, num, den, state, norm, out in (
        (phi_x, num_x, den_x, stx, nx, sx_ref),
        (phi_y, num_y, den_y, sty, ny, sy_ref),
    ):
        state_b = state[...].astype(BF)
        norm_row = norm[0:1, :]
        for piece in range(4):
            rows = slice(piece * 512, (piece + 1) * 512)
            phi_q = phi[rows, :]
            mixed = jnp.dot(phi_q.astype(BF), state_b, preferred_element_type=F32)
            top = num[rows, :] + mixed
            low = den[rows, :] + phi_q * norm_row
            out[rows, :] = (top / jnp.sum(low, axis=-1, keepdims=True)).astype(BF)


def teacher_kernel(
    tab, x_ref, y_ref, own, left, right, opp0, opp1, sx_ref, sy_ref,
    ox_ref, oy_ref, loss_ref, kv_s, part_ref, top_s, sum_s, acc_s, sems,
):
    chip = tab[16]
    far = 15 - chip
    copies = []
    for ref in (own, left, right, opp0, opp1):
        for i in range(ref.shape[0] // (2 * BLK)):
            slot = len(copies)
            copies.append(
                pltpu.make_async_copy(
                    ref.at[pl.ds(i * 2 * BLK, 2 * BLK), :],
                    kv_s.at[block_at(tab[slot], 2 * BLK), :],
                    sems.at[slot],
                )
            )
    for copy in copies:
        copy.start()
    unit = 1.4426950408889634 / 128**0.5
    part_ref[...] = jnp.zeros_like(part_ref)

    def tile(q_ref, piece, k, v, diagonal, first):
        rows = slice(piece * SUB, (piece + 1) * SUB)
        wide = k.shape[0] // 128
        s = lax.dot_general(q_ref[rows, :], k, NT, preferred_element_type=F32) * unit
        if diagonal:
            shape = (SUB, BLK)
            row = (lax.broadcasted_iota(jnp.int32, shape, 0) >> 3) + piece * (SUB // 8)
            last = jnp.where(row >= lax.broadcasted_iota(jnp.int32, shape, 1), s[:, -BLK:], -1e30)
            s = last if wide == 2 else jnp.concatenate([s[:, :-BLK], last], axis=1)
        peak = jnp.broadcast_to(jnp.max(s, axis=-1, keepdims=True), (SUB, 128))
        top = peak if first else jnp.maximum(top_s[rows, :], peak)
        p = jnp.exp2(s - jnp.concatenate([top] * wide, axis=1))
        added = p[:, :128]
        for i in range(1, wide):
            added = added + p[:, i * 128 : (i + 1) * 128]
        mixed = jnp.dot(p.astype(BF), v, preferred_element_type=F32)
        if first:
            sum_s[rows, :] = added
            acc_s[rows, :] = mixed
        else:
            keep = jnp.exp2(top_s[rows, :] - top)
            sum_s[rows, :] = sum_s[rows, :] * keep + added
            acc_s[rows, :] = acc_s[rows, :] * keep + mixed
        top_s[rows, :] = top

    def segment(q_ref, k, v, count, s_ref, o_ref):
        for piece in range(2):
            tile(q_ref, piece, k, v, True, True)

        def step(j, _):
            place = block_at(j, 2 * BLK)
            k, v = kv_s[place, :128], kv_s[place, 128:]
            for piece in range(2):
                tile(q_ref, piece, k, v, False, False)
            return 0

        lax.fori_loop(0, count, step, 0)
        for piece in range(2):
            rows = slice(piece * SUB, (piece + 1) * SUB)
            total = jnp.sum(sum_s[rows, :], axis=-1, keepdims=True)
            out = (acc_s[rows, :] / total).astype(BF)
            o_ref[rows, :] = out
            diff = out.astype(F32) - s_ref[rows, :].astype(F32)
            part_ref[...] += jnp.sum((diff * diff).reshape(SUB // 8, 8, 128), axis=0)

    for copy in copies:
        copy.wait()
    place = block_at(chip * 2)
    segment(x_ref, kv_s[place, :128], kv_s[place, 128:], chip, sx_ref, ox_ref)
    place = block_at(far, 2 * BLK)
    segment(y_ref, kv_s[place, :128], kv_s[place, 128:], far, sy_ref, oy_ref)
    loss_ref[...] = jnp.full_like(loss_ref, jnp.sum(part_ref[...]))


def assemble_kernel(tab, *refs):
    sources, outs, sems = (refs[:3], refs[3:6]), refs[6:8], refs[8]
    for core in range(2):

        @pl.when(tab[17] == core)
        def _(core=core):
            copies = []
            for k, ((near, came, distant), out) in enumerate(zip(sources, outs)):
                halves = (near, came) if core == 0 else (came, distant)
                for half, source in enumerate(halves):
                    target = out.at[:, pl.ds(half * 8, 8), :]
                    copies.append(pltpu.make_async_copy(source, target, sems.at[k * 2 + half]))
            for copy in copies:
                copy.start()
            for copy in copies:
                copy.wait()


def call(kernel, args, outs, scratch=(), flops=0, anywhere=(), limit=24, out_space=pltpu.VMEM):
    vmem = pl.BlockSpec(memory_space=pltpu.VMEM)
    specs = [
        pl.BlockSpec(memory_space=pltpu.SMEM)
        if i == 0
        else pl.BlockSpec(memory_space=pl.ANY)
        if i in anywhere
        else vmem
        for i in range(len(args))
    ]
    return pl.pallas_call(
        kernel,
        out_shape=[jax.ShapeDtypeStruct(shape, kind) for shape, kind in outs],
        in_specs=specs,
        out_specs=[pl.BlockSpec(memory_space=out_space)] * len(outs),
        scratch_shapes=list(scratch),
        compiler_params=pltpu.CompilerParams(vmem_limit_bytes=limit << 20),
        cost_estimate=pl.CostEstimate(flops=flops, bytes_accessed=1 << 20, transcendentals=0),
    )(*args)


def body(queries, keys, values, query_map, key_map):
    rows, heads, size = queries.shape
    core = lax.axis_index("c")
    chip = lax.axis_index("x") * 4 + lax.axis_index("y")
    first = core == 0
    pick = lambda a, b: jnp.where(first, a, b)

    kv = [jnp.concatenate([keys[:, g], values[:, g]], axis=1) for g in range(2)]
    kv_same, kv_other = pick(kv[0], kv[1]), pick(kv[1], kv[0])
    kv_came = permute(kv_other, SEQ, lambda r, c: (r, 1 - c))
    shard = jnp.concatenate([pick(kv_same, kv_came), pick(kv_came, kv_same)], axis=0)

    q = [queries[:, g * 8 : g * 8 + 8].reshape(8 * rows, size) for g in range(2)]
    q_same, q_other = lax.optimization_barrier((pick(q[0], q[1]), pick(q[1], q[0])))
    y_a = permute(q_other, SEQ, lambda r, c: None if c == 0 else (15 - r, 0))
    y_b = permute(q_same, SEQ, lambda r, c: None if c == 0 else (15 - r, 1))
    q_came = permute(q_other, SEQ, lambda r, c: (r, 1) if c == 0 else None)
    x = pick(q_same, q_came)
    y = pick(y_a, y_b)

    def shift(value, phase, by):
        def target(r, c):
            along_x = (c == 0) == (phase == 1)
            return (moved(r, by, 0) if along_x else moved(r, 0, by)), c

        return permute(value, SEQ, target)

    wk = lax.dynamic_index_in_dim(key_map, core, 0, keepdims=False).T
    wq = lax.dynamic_slice_in_dim(query_map, core * 8, 8, 0).transpose(0, 2, 1)
    many = x.shape
    inside = [(many, F32)] * 3
    wide = [pltpu.VMEM(many, F32)]
    states = [((128, 128), F32), ((128, 128), F32), ((8, 128), F32), ((8, 128), F32)]

    beside, across = shift(shard, 1, 1), shift(shard, 1, 3)
    near_pieces = [shard, beside, across, shift(across, 1, 1)]
    own = jnp.concatenate(near_pieces, axis=0)
    left, right = shift(own, 2, 1), shift(own, 2, 3)
    half = own.shape[0] // 2
    opp0 = shift(right[:half], 2, 1)
    opp1 = shift(left[half:], 2, 3)

    table = lax.dynamic_slice(
        jnp.asarray(TABLE.reshape(32, 16)), (chip * 2 + core, 0), (1, 16)
    ).reshape(16)
    table = jnp.concatenate([table, jnp.stack([chip, core]).astype(jnp.int32)])
    *near, stx, sty, nx, ny = call(
        near_kernel, (table, x, own, wk, wq), inside + states, wide, 2 << 30
    )
    *far, stx, sty, nx, ny = call(
        far_kernel,
        (table, y, left, right, wk, wq, stx, sty, nx, ny),
        inside + states,
        wide,
        2 << 30,
    )
    sx, sy = call(
        finish_kernel,
        (table, opp0, opp1, wk, stx, sty, nx, ny, *near, *far),
        [(many, BF)] * 2,
        [pltpu.VMEM(shape, kind) for shape, kind in states],
        flops=1 << 30,
    )

    def send_back(near, distant):
        came = permute(
            pick(distant, near), SEQ, lambda r, c: (r, 0) if c == 1 else (15 - r, 1)
        )
        came_far = permute(distant, SEQ, lambda r, c: None if c == 0 else (15 - r, 1))
        return came, came_far

    student_parts = (sx, *send_back(sx, sy))
    peers = 32 * lax.axis_size("h")
    ox, oy, part = call(
        teacher_kernel,
        (table, x, y, own, left, right, opp0, opp1, sx, sy),
        [(many, BF)] * 2 + [((peers, 1, 128), F32)],
        [pltpu.VMEM((16 * 2 * BLK, 256), BF), pltpu.VMEM((8, 128), F32)]
        + [pltpu.VMEM((2 * SUB, 128), F32)] * 3
        + [pltpu.SemaphoreType.DMA((16,))],
        flops=9 << 30,
        anywhere=(3, 4, 5, 6, 7),
        limit=32,
    )
    teacher_parts = (ox, *send_back(ox, oy))

    parts = lax.all_to_all(part, SEQ + ("h",), 0, 0, tiled=True)
    loss = jnp.sum(parts[:, 0, 0]) / (16 * 2 * rows * heads * lax.axis_size("h") * size)
    parts = [p.reshape(rows, 8, size) for p in teacher_parts + student_parts]
    teacher_attn, student_attn = call(
        assemble_kernel,
        (table, *parts),
        [((rows, heads, size), BF)] * 2,
        [pltpu.SemaphoreType.DMA((4,))],
        out_space=pl.ANY,
    )
    return teacher_attn, student_attn, loss


def solution(mesh):
    torus = Mesh(mesh.devices.reshape(4, 4, 2, mesh.shape["head"]), ("x", "y", "c", "h"))
    return jax.shard_map(
        body,
        mesh=torus,
        in_specs=(
            P(SEQ, "h", None),
            P(SEQ, "h", None),
            P(SEQ, "h", None),
            P("h", None, None),
            P("h", None, None),
        ),
        out_specs=(P(SEQ, "h", None), P(SEQ, "h", None), P()),
        check_vma=False,
    )
```

```python
import jax
import jax.numpy as jnp
import numpy as np
from jax import lax
from jax.experimental import pallas as pl
from jax.experimental.pallas import tpu as pltpu
from jax.sharding import Mesh
from jax.sharding import PartitionSpec as P


SEQ = ("x", "y", "c")
BF = jnp.bfloat16
F32 = jnp.float32
NT = (((1,), (1,)), ((), ()))
BLK = 256
SUB = 1024

MASKS = (0, 1, 3, 2)


def moved(chip, mx, my):
    return chip ^ (mx * 4 + my)


def slot_table():
    table = np.zeros((16, 2, 16), np.int32)
    for chip in range(16):
        for slot in range(16):
            one, two = MASKS[slot % 4], MASKS[slot // 4]
            for core, (mx, my) in enumerate(((one, two), (two, one))):
                table[chip, core, slot] = moved(chip, mx, my)
    return table


TABLE = slot_table()


def permute(value, axes, target):
    pairs = []
    for chip in range(16):
        for core in range(2):
            to = target(chip, core)
            if to is not None:
                pairs.append((chip * 2 + core, to[0] * 2 + to[1]))
    return lax.ppermute(value, axes, pairs)


def features(mapped):
    high = jnp.max(mapped, axis=0, keepdims=True)
    low = jnp.min(mapped, axis=0, keepdims=True)
    up = jnp.exp(mapped - high)
    down = jnp.exp(low - mapped)
    up = up * (1.0 / jnp.sum(up, axis=0, keepdims=True))
    down = down * (1.0 / jnp.sum(down, axis=0, keepdims=True))
    return jnp.concatenate([up, down], axis=0).astype(BF)


def block_at(index, size=BLK):
    return pl.ds(pl.multiple_of(index * size, size), size)


def student_inside(q_ref, keys, values, wk, wq, phi_ref, num_ref, den_ref, wide_s):
    wide_s[...] = q_ref[: 8 * BLK, :].astype(F32)
    phi_k = features(lax.dot_general(wk[...], keys, NT, preferred_element_type=F32))
    rows = lax.broadcasted_iota(jnp.int32, (BLK, BLK), 0)
    cols = lax.broadcasted_iota(jnp.int32, (BLK, BLK), 1)

    def head(h, _):
        place = pl.ds(h, BLK, stride=8)
        q = wide_s[place, :].astype(BF)
        mapped = lax.dot_general(wq[h], q, NT, preferred_element_type=F32)
        phi_q = features(mapped).T
        inner = jnp.dot(phi_q, phi_k, preferred_element_type=F32)
        inner = jnp.where(rows >= cols, inner, 0.0)
        phi_ref[place, :] = phi_q.astype(F32)
        num_ref[place, :] = jnp.dot(inner.astype(BF), values, preferred_element_type=F32)
        den_ref[place, :] = inner[:, :128] + inner[:, 128:]
        return 0

    lax.fori_loop(0, 8, head, 0, unroll=2)


def add_state(tab, wk, slot, kv, stx, sty, nx, ny):
    chip = tab[16]
    far = 15 - chip
    other = tab[slot]
    ones = jnp.ones((8, BLK), BF)
    phi = features(lax.dot_general(wk[...], kv[:, :128], NT, preferred_element_type=F32))
    phi_a, phi_b = phi[:, :BLK], phi[:, BLK:]
    state_a = jnp.dot(phi_a, kv[:BLK, 128:], preferred_element_type=F32)
    state_b = jnp.dot(phi_b, kv[BLK:, 128:], preferred_element_type=F32)
    norm_a = lax.dot_general(ones, phi_a, NT, preferred_element_type=F32)
    norm_b = lax.dot_general(ones, phi_b, NT, preferred_element_type=F32)
    in_x = jnp.where(other < chip, 1.0, 0.0).astype(F32)
    in_ya = jnp.where(other <= far, 1.0, 0.0).astype(F32)
    in_yb = jnp.where(other < far, 1.0, 0.0).astype(F32)
    stx[...] += in_x * (state_a + state_b)
    nx[...] += in_x * (norm_a + norm_b)
    sty[...] += in_ya * state_a + in_yb * state_b
    ny[...] += in_ya * norm_a + in_yb * norm_b


def near_kernel(
    tab, x_ref, own, wk, wq, phi_ref, num_ref, den_ref, stx, sty, nx, ny, wide_s
):
    for ref in (stx, sty, nx, ny):
        ref[...] = jnp.zeros_like(ref)
    for i in range(4):
        add_state(tab, wk, i, own[i * 2 * BLK : (i + 1) * 2 * BLK, :], stx, sty, nx, ny)
    keys, values = own[:BLK, :128], own[:BLK, 128:]
    student_inside(x_ref, keys, values, wk, wq, phi_ref, num_ref, den_ref, wide_s)


def far_kernel(
    tab, y_ref, left, right, wk, wq, stx0, sty0, nx0, ny0,
    phi_ref, num_ref, den_ref, stx, sty, nx, ny, wide_s,
):
    own = slice(5 * BLK, 6 * BLK)
    keys, values = right[own, :128], right[own, 128:]
    student_inside(y_ref, keys, values, wk, wq, phi_ref, num_ref, den_ref, wide_s)
    for ref, start in ((stx, stx0), (sty, sty0), (nx, nx0), (ny, ny0)):
        ref[...] = start[...]
    for group, ref in enumerate((left, right)):
        for i in range(4):
            kv = ref[i * 2 * BLK : (i + 1) * 2 * BLK, :]
            add_state(tab, wk, 4 + group * 4 + i, kv, stx, sty, nx, ny)


def finish_kernel(
    tab, opp0, opp1, wk, stx0, sty0, nx0, ny0, phi_x, num_x, den_x, phi_y, num_y, den_y,
    sx_ref, sy_ref, stx, sty, nx, ny,
):
    for ref, start in ((stx, stx0), (sty, sty0), (nx, nx0), (ny, ny0)):
        ref[...] = start[...]
    for group, ref in enumerate((opp0, opp1)):
        for i in range(2):
            kv = ref[i * 2 * BLK : (i + 1) * 2 * BLK, :]
            add_state(tab, wk, 12 + group * 2 + i, kv, stx, sty, nx, ny)
    for phi, num, den, state, norm, out in (
        (phi_x, num_x, den_x, stx, nx, sx_ref),
        (phi_y, num_y, den_y, sty, ny, sy_ref),
    ):
        state_b = state[...].astype(BF)
        norm_row = norm[0:1, :]
        for piece in range(4):
            rows = slice(piece * 512, (piece + 1) * 512)
            phi_q = phi[rows, :]
            mixed = jnp.dot(phi_q.astype(BF), state_b, preferred_element_type=F32)
            top = num[rows, :] + mixed
            low = den[rows, :] + phi_q * norm_row
            out[rows, :] = (top / jnp.sum(low, axis=-1, keepdims=True)).astype(BF)


def teacher_kernel(
    tab, x_ref, y_ref, own, left, right, opp0, opp1, sx_ref, sy_ref,
    ox_ref, oy_ref, loss_ref, kv_s, q_s, part_ref, top_s, sum_s, acc_s, sems,
):
    chip = tab[16]
    far = 15 - chip
    copies = []
    for ref in (own, left, right, opp0, opp1):
        for i in range(ref.shape[0] // (2 * BLK)):
            slot = len(copies)
            copies.append(
                pltpu.make_async_copy(
                    ref.at[pl.ds(i * 2 * BLK, 2 * BLK), :],
                    kv_s.at[block_at(tab[slot], 2 * BLK), :],
                    sems.at[slot],
                )
            )
    for copy in copies:
        copy.start()
    unit = 1.4426950408889634 / 128**0.5
    part_ref[...] = jnp.zeros_like(part_ref)

    for index, ref in enumerate((x_ref, y_ref)):
        scaled = ref[...].astype(F32) * unit
        high = scaled.astype(BF)
        q_s[index, :, :128] = high
        q_s[index, :, 128:] = (scaled - high.astype(F32)).astype(BF)

    def tile(index, piece, place, diagonal, first):
        rows = slice(piece * SUB, (piece + 1) * SUB)
        k, v = kv_s[place, :128], kv_s[place, 128:]
        wide = k.shape[0] // 128
        twice = jnp.concatenate([k, k], axis=1)
        s = lax.dot_general(q_s[index, rows, :], twice, NT, preferred_element_type=F32)
        if diagonal:
            shape = (SUB, BLK)
            row = (lax.broadcasted_iota(jnp.int32, shape, 0) >> 3) + piece * (SUB // 8)
            last = jnp.where(row >= lax.broadcasted_iota(jnp.int32, shape, 1), s[:, -BLK:], -1e30)
            s = last if wide == 2 else jnp.concatenate([s[:, :-BLK], last], axis=1)
        peak = jnp.broadcast_to(jnp.max(s, axis=-1, keepdims=True), (SUB, 128))
        top = peak if first else jnp.maximum(top_s[rows, :], peak)
        p = jnp.exp2(s - jnp.concatenate([top] * wide, axis=1))
        added = p[:, :128]
        for i in range(1, wide):
            added = added + p[:, i * 128 : (i + 1) * 128]
        mixed = jnp.dot(p.astype(BF), v, preferred_element_type=F32)
        if first:
            sum_s[rows, :] = added
            acc_s[rows, :] = mixed
        else:
            keep = jnp.exp2(top_s[rows, :] - top)
            sum_s[rows, :] = sum_s[rows, :] * keep + added
            acc_s[rows, :] = acc_s[rows, :] * keep + mixed
        top_s[rows, :] = top

    def both(index, place, diagonal=False, first=False):
        for piece in range(2):
            tile(index, piece, place, diagonal, first)

    def segment(index, count, s_ref, o_ref):
        def step(j, _):
            both(index, block_at(j, 4 * BLK))
            return 0

        lax.fori_loop(0, count // 2, step, 0)

        @pl.when(count % 2 == 1)
        def _():
            both(index, block_at(count - 1, 2 * BLK))

        for piece in range(2):
            rows = slice(piece * SUB, (piece + 1) * SUB)
            total = jnp.sum(sum_s[rows, :], axis=-1, keepdims=True)
            out = (acc_s[rows, :] / total).astype(BF)
            o_ref[rows, :] = out
            diff = out.astype(F32) - s_ref[rows, :].astype(F32)
            part_ref[...] += jnp.sum((diff * diff).reshape(SUB // 8, 8, 128), axis=0)

    copies[0].wait()
    both(0, block_at(chip * 2), True, True)
    for copy in copies[1:]:
        copy.wait()
    segment(0, chip, sx_ref, ox_ref)
    both(1, block_at(far, 2 * BLK), True, True)
    segment(1, far, sy_ref, oy_ref)
    loss_ref[...] = jnp.full_like(loss_ref, jnp.sum(part_ref[...]))


def assemble_kernel(tab, *refs):
    sources, parts, outs, loss_ref, sems = (refs[:3], refs[3:6]), refs[6], refs[7:9], *refs[9:]
    loss_ref[0, 0] = jnp.sum(parts[...]) * (1.0 / (128 * outs[0].size * 128))
    for core in range(2):

        @pl.when(tab[17] == core)
        def _(core=core):
            copies = []
            for k, ((near, came, distant), out) in enumerate(zip(sources, outs)):
                halves = (near, came) if core == 0 else (came, distant)
                for half, source in enumerate(halves):
                    target = out.at[:, pl.ds(half * 8, 8), :]
                    copies.append(pltpu.make_async_copy(source, target, sems.at[k * 2 + half]))
            for copy in copies:
                copy.start()
            for copy in copies:
                copy.wait()


def call(kernel, args, outs, scratch=(), flops=0, anywhere=(), limit=24, out_space=None):
    vmem = pl.BlockSpec(memory_space=pltpu.VMEM)
    specs = [
        pl.BlockSpec(memory_space=pltpu.SMEM)
        if i == 0
        else pl.BlockSpec(memory_space=pl.ANY)
        if i in anywhere
        else vmem
        for i in range(len(args))
    ]
    return pl.pallas_call(
        kernel,
        out_shape=[jax.ShapeDtypeStruct(shape, kind) for shape, kind in outs],
        in_specs=specs,
        out_specs=[pl.BlockSpec(memory_space=m) for m in out_space or [pltpu.VMEM] * len(outs)],
        scratch_shapes=list(scratch),
        compiler_params=pltpu.CompilerParams(vmem_limit_bytes=limit << 20),
        cost_estimate=pl.CostEstimate(flops=flops, bytes_accessed=1 << 20, transcendentals=0),
    )(*args)


def body(queries, keys, values, query_map, key_map):
    rows, heads, size = queries.shape
    core = lax.axis_index("c")
    chip = lax.axis_index("x") * 4 + lax.axis_index("y")
    first = core == 0
    pick = lambda a, b: jnp.where(first, a, b)

    kv = [jnp.concatenate([keys[:, g], values[:, g]], axis=1) for g in range(2)]
    kv_same, kv_other = pick(kv[0], kv[1]), pick(kv[1], kv[0])
    kv_came = permute(kv_other, SEQ, lambda r, c: (r, 1 - c))
    shard = jnp.concatenate([pick(kv_same, kv_came), pick(kv_came, kv_same)], axis=0)

    q = [queries[:, g * 8 : g * 8 + 8].reshape(8 * rows, size) for g in range(2)]
    q_same, q_other = lax.optimization_barrier((pick(q[0], q[1]), pick(q[1], q[0])))
    y_a = permute(q_other, SEQ, lambda r, c: None if c == 0 else (15 - r, 0))
    y_b = permute(q_same, SEQ, lambda r, c: None if c == 0 else (15 - r, 1))
    q_came = permute(q_other, SEQ, lambda r, c: (r, 1) if c == 0 else None)
    x = pick(q_same, q_came)
    y = pick(y_a, y_b)

    def shift(value, phase, by):
        def target(r, c):
            along_x = (c == 0) == (phase == 1)
            return (moved(r, by, 0) if along_x else moved(r, 0, by)), c

        return permute(value, SEQ, target)

    wk = lax.dynamic_index_in_dim(key_map, core, 0, keepdims=False).T
    wq = lax.dynamic_slice_in_dim(query_map, core * 8, 8, 0).transpose(0, 2, 1)
    many = x.shape
    inside = [(many, F32)] * 3
    wide = [pltpu.VMEM(many, F32)]
    states = [((128, 128), F32), ((128, 128), F32), ((8, 128), F32), ((8, 128), F32)]

    beside, across = shift(shard, 1, 1), shift(shard, 1, 3)
    near_pieces = [shard, beside, across, shift(across, 1, 1)]
    own = jnp.concatenate(near_pieces, axis=0)
    left, right = shift(own, 2, 1), shift(own, 2, 3)
    half = own.shape[0] // 2
    opp0 = shift(right[:half], 2, 1)
    opp1 = shift(left[half:], 2, 3)

    table = lax.dynamic_slice(
        jnp.asarray(TABLE.reshape(32, 16)), (chip * 2 + core, 0), (1, 16)
    ).reshape(16)
    table = jnp.concatenate([table, jnp.stack([chip, core]).astype(jnp.int32)])
    *near, stx, sty, nx, ny = call(
        near_kernel, (table, x, own, wk, wq), inside + states, wide, 2 << 30
    )
    *far, stx, sty, nx, ny = call(
        far_kernel,
        (table, y, left, right, wk, wq, stx, sty, nx, ny),
        inside + states,
        wide,
        2 << 30,
    )
    sx, sy = call(
        finish_kernel,
        (table, opp0, opp1, wk, stx, sty, nx, ny, *near, *far),
        [(many, BF)] * 2,
        [pltpu.VMEM(shape, kind) for shape, kind in states],
        flops=1 << 30,
    )

    def send_back(near, distant):
        came = permute(
            pick(distant, near), SEQ, lambda r, c: (r, 0) if c == 1 else (15 - r, 1)
        )
        came_far = permute(distant, SEQ, lambda r, c: None if c == 0 else (15 - r, 1))
        return came, came_far

    student_parts = (sx, *send_back(sx, sy))
    peers = 32 * lax.axis_size("h")
    ox, oy, part = call(
        teacher_kernel,
        (table, x, y, own, left, right, opp0, opp1, sx, sy),
        [(many, BF)] * 2 + [((peers, 1, 128), F32)],
        [
            pltpu.VMEM((16 * 2 * BLK, 256), BF),
            pltpu.VMEM((2, 2 * SUB, 256), BF),
            pltpu.VMEM((8, 128), F32),
        ]
        + [pltpu.VMEM((2 * SUB, 128), F32)] * 3
        + [pltpu.SemaphoreType.DMA((16,))],
        flops=9 << 30,
        anywhere=(3, 4, 5, 6, 7),
        limit=32,
    )
    teacher_parts = (ox, *send_back(ox, oy))

    parts = lax.all_to_all(part, SEQ + ("h",), 0, 0, tiled=True)
    pieces = [p.reshape(rows, 8, size) for p in teacher_parts + student_parts]
    teacher_attn, student_attn, loss = call(
        assemble_kernel,
        (table, *pieces, parts),
        [((rows, heads, size), BF)] * 2 + [((1, 1), F32)],
        [pltpu.SemaphoreType.DMA((4,))],
        out_space=[pl.ANY, pl.ANY, pltpu.SMEM],
    )
    return teacher_attn, student_attn, loss.reshape(())


def solution(mesh):
    torus = Mesh(mesh.devices.reshape(4, 4, 2, mesh.shape["head"]), ("x", "y", "c", "h"))
    return jax.shard_map(
        body,
        mesh=torus,
        in_specs=(
            P(SEQ, "h", None),
            P(SEQ, "h", None),
            P(SEQ, "h", None),
            P("h", None, None),
            P("h", None, None),
        ),
        out_specs=(P(SEQ, "h", None), P(SEQ, "h", None), P()),
        check_vma=False,
    )
```

```python
import jax
import jax.numpy as jnp
import numpy as np
from jax import lax
from jax.experimental import pallas as pl
from jax.experimental.pallas import tpu as pltpu
from jax.sharding import Mesh
from jax.sharding import PartitionSpec as P


SEQ = ("x", "y", "c")
BF = jnp.bfloat16
F32 = jnp.float32
NT = (((1,), (1,)), ((), ()))
BLK = 256
SUB = 2048

MASKS = (0, 1, 3, 2)


def moved(chip, mx, my):
    return chip ^ (mx * 4 + my)


def slot_table():
    table = np.zeros((16, 2, 16), np.int32)
    for chip in range(16):
        for slot in range(16):
            one, two = MASKS[slot % 4], MASKS[slot // 4]
            for core, (mx, my) in enumerate(((one, two), (two, one))):
                table[chip, core, slot] = moved(chip, mx, my)
    return table


TABLE = slot_table()


def permute(value, axes, target):
    pairs = []
    for chip in range(16):
        for core in range(2):
            to = target(chip, core)
            if to is not None:
                pairs.append((chip * 2 + core, to[0] * 2 + to[1]))
    return lax.ppermute(value, axes, pairs)


def features(mapped):
    high = jnp.max(mapped, axis=0, keepdims=True)
    low = jnp.min(mapped, axis=0, keepdims=True)
    up = jnp.exp(mapped - high)
    down = jnp.exp(low - mapped)
    up = up * (1.0 / jnp.sum(up, axis=0, keepdims=True))
    down = down * (1.0 / jnp.sum(down, axis=0, keepdims=True))
    return jnp.concatenate([up, down], axis=0).astype(BF)


def block_at(index, size=BLK):
    return pl.ds(pl.multiple_of(index * size, size), size)


def student_inside(q_ref, keys, values, wk, wq, phi_ref, num_ref, den_ref, wide_s):
    wide_s[...] = q_ref[: 8 * BLK, :].astype(F32)
    phi_k = features(lax.dot_general(wk[...], keys, NT, preferred_element_type=F32))
    rows = lax.broadcasted_iota(jnp.int32, (BLK, BLK), 0)
    cols = lax.broadcasted_iota(jnp.int32, (BLK, BLK), 1)

    def head(h, _):
        place = pl.ds(h, BLK, stride=8)
        q = wide_s[place, :].astype(BF)
        mapped = lax.dot_general(wq[h], q, NT, preferred_element_type=F32)
        phi_q = features(mapped).T
        inner = jnp.dot(phi_q, phi_k, preferred_element_type=F32)
        inner = jnp.where(rows >= cols, inner, 0.0)
        phi_ref[place, :] = phi_q.astype(F32)
        num_ref[place, :] = jnp.dot(inner.astype(BF), values, preferred_element_type=F32)
        den_ref[place, :] = inner[:, :128] + inner[:, 128:]
        return 0

    lax.fori_loop(0, 8, head, 0, unroll=2)


def add_state(tab, wk, slot, kv, stx, sty, nx, ny):
    chip = tab[16]
    far = 15 - chip
    other = tab[slot]
    ones = jnp.ones((8, BLK), BF)
    phi = features(lax.dot_general(wk[...], kv[:, :128], NT, preferred_element_type=F32))
    phi_a, phi_b = phi[:, :BLK], phi[:, BLK:]
    state_a = jnp.dot(phi_a, kv[:BLK, 128:], preferred_element_type=F32)
    state_b = jnp.dot(phi_b, kv[BLK:, 128:], preferred_element_type=F32)
    norm_a = lax.dot_general(ones, phi_a, NT, preferred_element_type=F32)
    norm_b = lax.dot_general(ones, phi_b, NT, preferred_element_type=F32)
    in_x = jnp.where(other < chip, 1.0, 0.0).astype(F32)
    in_ya = jnp.where(other <= far, 1.0, 0.0).astype(F32)
    in_yb = jnp.where(other < far, 1.0, 0.0).astype(F32)
    stx[...] += in_x * (state_a + state_b)
    nx[...] += in_x * (norm_a + norm_b)
    sty[...] += in_ya * state_a + in_yb * state_b
    ny[...] += in_ya * norm_a + in_yb * norm_b


def near_kernel(
    tab, x_ref, own, wk, wq, phi_ref, num_ref, den_ref, stx, sty, nx, ny, wide_s
):
    for ref in (stx, sty, nx, ny):
        ref[...] = jnp.zeros_like(ref)
    for i in range(4):
        add_state(tab, wk, i, own[i * 2 * BLK : (i + 1) * 2 * BLK, :], stx, sty, nx, ny)
    keys, values = own[:BLK, :128], own[:BLK, 128:]
    student_inside(x_ref, keys, values, wk, wq, phi_ref, num_ref, den_ref, wide_s)


def far_kernel(
    tab, y_ref, left, right, wk, wq, stx0, sty0, nx0, ny0,
    phi_ref, num_ref, den_ref, stx, sty, nx, ny, wide_s,
):
    own = slice(5 * BLK, 6 * BLK)
    keys, values = right[own, :128], right[own, 128:]
    student_inside(y_ref, keys, values, wk, wq, phi_ref, num_ref, den_ref, wide_s)
    for ref, start in ((stx, stx0), (sty, sty0), (nx, nx0), (ny, ny0)):
        ref[...] = start[...]
    for group, ref in enumerate((left, right)):
        for i in range(4):
            kv = ref[i * 2 * BLK : (i + 1) * 2 * BLK, :]
            add_state(tab, wk, 4 + group * 4 + i, kv, stx, sty, nx, ny)


def finish_kernel(
    tab, opp0, opp1, wk, stx0, sty0, nx0, ny0, phi_x, num_x, den_x, phi_y, num_y, den_y,
    sx_ref, sy_ref, stx, sty, nx, ny,
):
    for ref, start in ((stx, stx0), (sty, sty0), (nx, nx0), (ny, ny0)):
        ref[...] = start[...]
    for group, ref in enumerate((opp0, opp1)):
        for i in range(2):
            kv = ref[i * 2 * BLK : (i + 1) * 2 * BLK, :]
            add_state(tab, wk, 12 + group * 2 + i, kv, stx, sty, nx, ny)
    for phi, num, den, state, norm, out in (
        (phi_x, num_x, den_x, stx, nx, sx_ref),
        (phi_y, num_y, den_y, sty, ny, sy_ref),
    ):
        state_b = state[...].astype(BF)
        norm_row = norm[0:1, :]
        for piece in range(4):
            rows = slice(piece * 512, (piece + 1) * 512)
            phi_q = phi[rows, :]
            mixed = jnp.dot(phi_q.astype(BF), state_b, preferred_element_type=F32)
            top = num[rows, :] + mixed
            low = den[rows, :] + phi_q * norm_row
            out[rows, :] = (top / jnp.sum(low, axis=-1, keepdims=True)).astype(BF)


def teacher_kernel(
    tab, x_ref, y_ref, own, left, right, opp0, opp1, sx_ref, sy_ref,
    ox_ref, oy_ref, loss_ref, kv_s, q_s, part_ref, top_s, sum_s, acc_s, sems,
):
    chip = tab[16]
    far = 15 - chip
    copies = []
    for ref in (own, left, right, opp0, opp1):
        for i in range(ref.shape[0] // (2 * BLK)):
            slot = len(copies)
            copies.append(
                pltpu.make_async_copy(
                    ref.at[pl.ds(i * 2 * BLK, 2 * BLK), :],
                    kv_s.at[block_at(tab[slot], 2 * BLK), :],
                    sems.at[slot],
                )
            )
    for copy in copies:
        copy.start()
    unit = 1.4426950408889634 / 128**0.5
    part_ref[...] = jnp.zeros_like(part_ref)

    for index, ref in enumerate((x_ref, y_ref)):
        scaled = ref[...].astype(F32) * unit
        high = scaled.astype(BF)
        q_s[index, :, :128] = high
        q_s[index, :, 128:] = (scaled - high.astype(F32)).astype(BF)

    def tile(index, piece, place, diagonal, first):
        rows = slice(piece * SUB, (piece + 1) * SUB)
        k, v = kv_s[place, :128], kv_s[place, 128:]
        wide = k.shape[0] // 128
        twice = jnp.concatenate([k, k], axis=1)
        s = lax.dot_general(q_s[index, rows, :], twice, NT, preferred_element_type=F32)
        if diagonal:
            shape = (SUB, BLK)
            row = (lax.broadcasted_iota(jnp.int32, shape, 0) >> 3) + piece * (SUB // 8)
            last = jnp.where(row >= lax.broadcasted_iota(jnp.int32, shape, 1), s[:, -BLK:], -1e30)
            s = last if wide == 2 else jnp.concatenate([s[:, :-BLK], last], axis=1)
        peak = jnp.broadcast_to(jnp.max(s, axis=-1, keepdims=True), (SUB, 128))
        top = peak if first else jnp.maximum(top_s[rows, :], peak)
        p = jnp.exp2(s - jnp.concatenate([top] * wide, axis=1))
        added = p[:, :128]
        for i in range(1, wide):
            added = added + p[:, i * 128 : (i + 1) * 128]
        mixed = jnp.dot(p.astype(BF), v, preferred_element_type=F32)
        if first:
            sum_s[rows, :] = added
            acc_s[rows, :] = mixed
        else:
            keep = jnp.exp2(top_s[rows, :] - top)
            sum_s[rows, :] = sum_s[rows, :] * keep + added
            acc_s[rows, :] = acc_s[rows, :] * keep + mixed
        top_s[rows, :] = top

    def both(index, place, diagonal=False, first=False):
        for piece in range(8 * BLK // SUB):
            tile(index, piece, place, diagonal, first)

    def segment(index, count, s_ref, o_ref):
        def step(j, _):
            both(index, block_at(j, 4 * BLK))
            return 0

        lax.fori_loop(0, count // 2, step, 0)

        @pl.when(count % 2 == 1)
        def _():
            both(index, block_at(count - 1, 2 * BLK))

        for piece in range(8 * BLK // SUB):
            rows = slice(piece * SUB, (piece + 1) * SUB)
            total = jnp.sum(sum_s[rows, :], axis=-1, keepdims=True)
            out = (acc_s[rows, :] / total).astype(BF)
            o_ref[rows, :] = out
            diff = out.astype(F32) - s_ref[rows, :].astype(F32)
            part_ref[...] += jnp.sum((diff * diff).reshape(SUB // 8, 8, 128), axis=0)

    copies[0].wait()
    both(0, block_at(chip * 2), True, True)
    for copy in copies[1:]:
        copy.wait()
    segment(0, chip, sx_ref, ox_ref)
    both(1, block_at(far, 2 * BLK), True, True)
    segment(1, far, sy_ref, oy_ref)
    loss_ref[...] = jnp.full_like(loss_ref, jnp.sum(part_ref[...]))


def assemble_kernel(tab, *refs):
    sources, parts, outs, loss_ref, sems = (refs[:3], refs[3:6]), refs[6], refs[7:9], *refs[9:]
    loss_ref[0, 0] = jnp.sum(parts[...]) * (1.0 / (128 * outs[0].size * 128))
    for core in range(2):

        @pl.when(tab[17] == core)
        def _(core=core):
            copies = []
            for k, ((near, came, distant), out) in enumerate(zip(sources, outs)):
                halves = (near, came) if core == 0 else (came, distant)
                for half, source in enumerate(halves):
                    target = out.at[:, pl.ds(half * 8, 8), :]
                    copies.append(pltpu.make_async_copy(source, target, sems.at[k * 2 + half]))
            for copy in copies:
                copy.start()
            for copy in copies:
                copy.wait()


def call(kernel, args, outs, scratch=(), flops=0, anywhere=(), limit=24, out_space=None):
    vmem = pl.BlockSpec(memory_space=pltpu.VMEM)
    specs = [
        pl.BlockSpec(memory_space=pltpu.SMEM)
        if i == 0
        else pl.BlockSpec(memory_space=pl.ANY)
        if i in anywhere
        else vmem
        for i in range(len(args))
    ]
    return pl.pallas_call(
        kernel,
        out_shape=[jax.ShapeDtypeStruct(shape, kind) for shape, kind in outs],
        in_specs=specs,
        out_specs=[pl.BlockSpec(memory_space=m) for m in out_space or [pltpu.VMEM] * len(outs)],
        scratch_shapes=list(scratch),
        compiler_params=pltpu.CompilerParams(vmem_limit_bytes=limit << 20),
        cost_estimate=pl.CostEstimate(flops=flops, bytes_accessed=1 << 20, transcendentals=0),
    )(*args)


def body(queries, keys, values, query_map, key_map):
    rows, heads, size = queries.shape
    core = lax.axis_index("c")
    chip = lax.axis_index("x") * 4 + lax.axis_index("y")
    first = core == 0
    pick = lambda a, b: jnp.where(first, a, b)

    kv = [jnp.concatenate([keys[:, g], values[:, g]], axis=1) for g in range(2)]
    kv_same, kv_other = pick(kv[0], kv[1]), pick(kv[1], kv[0])
    kv_came = permute(kv_other, SEQ, lambda r, c: (r, 1 - c))
    shard = jnp.concatenate([pick(kv_same, kv_came), pick(kv_came, kv_same)], axis=0)

    q = [queries[:, g * 8 : g * 8 + 8].reshape(8 * rows, size) for g in range(2)]
    q_same, q_other = lax.optimization_barrier((pick(q[0], q[1]), pick(q[1], q[0])))
    y_a = permute(q_other, SEQ, lambda r, c: None if c == 0 else (15 - r, 0))
    y_b = permute(q_same, SEQ, lambda r, c: None if c == 0 else (15 - r, 1))
    q_came = permute(q_other, SEQ, lambda r, c: (r, 1) if c == 0 else None)
    x = pick(q_same, q_came)
    y = pick(y_a, y_b)

    def shift(value, phase, by):
        def target(r, c):
            along_x = (c == 0) == (phase == 1)
            return (moved(r, by, 0) if along_x else moved(r, 0, by)), c

        return permute(value, SEQ, target)

    wk = lax.dynamic_index_in_dim(key_map, core, 0, keepdims=False).T
    wq = lax.dynamic_slice_in_dim(query_map, core * 8, 8, 0).transpose(0, 2, 1)
    many = x.shape
    inside = [(many, F32)] * 3
    wide = [pltpu.VMEM(many, F32)]
    states = [((128, 128), F32), ((128, 128), F32), ((8, 128), F32), ((8, 128), F32)]

    beside, across = shift(shard, 1, 1), shift(shard, 1, 3)
    near_pieces = [shard, beside, across, shift(across, 1, 1)]
    own = jnp.concatenate(near_pieces, axis=0)
    left, right = shift(own, 2, 1), shift(own, 2, 3)
    half = own.shape[0] // 2
    opp0 = shift(right[:half], 2, 1)
    opp1 = shift(left[half:], 2, 3)

    table = lax.dynamic_slice(
        jnp.asarray(TABLE.reshape(32, 16)), (chip * 2 + core, 0), (1, 16)
    ).reshape(16)
    table = jnp.concatenate([table, jnp.stack([chip, core]).astype(jnp.int32)])
    *near, stx, sty, nx, ny = call(
        near_kernel, (table, x, own, wk, wq), inside + states, wide, 2 << 30
    )
    *far, stx, sty, nx, ny = call(
        far_kernel,
        (table, y, left, right, wk, wq, stx, sty, nx, ny),
        inside + states,
        wide,
        2 << 30,
    )
    sx, sy = call(
        finish_kernel,
        (table, opp0, opp1, wk, stx, sty, nx, ny, *near, *far),
        [(many, BF)] * 2,
        [pltpu.VMEM(shape, kind) for shape, kind in states],
        flops=1 << 30,
    )

    def send_back(near, distant):
        came = permute(
            pick(distant, near), SEQ, lambda r, c: (r, 0) if c == 1 else (15 - r, 1)
        )
        came_far = permute(distant, SEQ, lambda r, c: None if c == 0 else (15 - r, 1))
        return came, came_far

    student_parts = (sx, *send_back(sx, sy))
    peers = 32 * lax.axis_size("h")
    ox, oy, part = call(
        teacher_kernel,
        (table, x, y, own, left, right, opp0, opp1, sx, sy),
        [(many, BF)] * 2 + [((peers, 1, 128), F32)],
        [
            pltpu.VMEM((16 * 2 * BLK, 256), BF),
            pltpu.VMEM((2, SUB, 256), BF),
            pltpu.VMEM((8, 128), F32),
        ]
        + [pltpu.VMEM((SUB, 128), F32)] * 3
        + [pltpu.SemaphoreType.DMA((16,))],
        flops=9 << 30,
        anywhere=(3, 4, 5, 6, 7),
        limit=32,
    )
    teacher_parts = (ox, *send_back(ox, oy))

    parts = lax.all_to_all(part, SEQ + ("h",), 0, 0, tiled=True)
    pieces = [p.reshape(rows, 8, size) for p in teacher_parts + student_parts]
    teacher_attn, student_attn, loss = call(
        assemble_kernel,
        (table, *pieces, parts),
        [((rows, heads, size), BF)] * 2 + [((1, 1), F32)],
        [pltpu.SemaphoreType.DMA((4,))],
        out_space=[pl.ANY, pl.ANY, pltpu.SMEM],
    )
    return teacher_attn, student_attn, loss.reshape(())


def solution(mesh):
    torus = Mesh(mesh.devices.reshape(4, 4, 2, mesh.shape["head"]), ("x", "y", "c", "h"))
    return jax.shard_map(
        body,
        mesh=torus,
        in_specs=(
            P(SEQ, "h", None),
            P(SEQ, "h", None),
            P(SEQ, "h", None),
            P("h", None, None),
            P("h", None, None),
        ),
        out_specs=(P(SEQ, "h", None), P(SEQ, "h", None), P()),
        check_vma=False,
    )
```
